32 devices in a mesh: dp: 2 (over y), seq: 8 (over z, x), head: 2 (over core).
Axes of the slice: x: 2, y: 2, z: 4, core: 2. Of those that a mesh axis runs over, the one named last changes fastest.
Arguments:
- queries: bfloat16 [128, 8, 1024], P('seq', 'dp', 'head'), parts along dimension 1, may hold values from -6 to 6
- gate_pre: bfloat16 [128, 8, 1024], P('seq', 'dp', 'head'), parts along dimension 1, may hold values from -6 to 6
- event_keys: bfloat16 [8192, 8, 1024], P('seq', 'dp', 'head'), parts along dimension 1, may hold values from -6 to 6
- event_values: bfloat16 [8192, 8, 1024], P('seq', 'dp', 'head'), parts along dimension 1, may hold values from -6 to 6
- block_lists: int32 [8, 8, 4], P(None, 'dp'), parts along dimension 1, may hold values from 0 to 7, all different within a row; in each aligned block of 4 rows (0 to 3, 4 to 7, ..., all dimensions but the last counted through in order) at most 2 rows name the same one
- history_len: int32 [8], P('dp'), parts along dimension 0, may hold values from 4 to 8
- out_grad: bfloat16 [128, 8, 1024], P('seq', 'dp', 'head'), parts along dimension 1, may hold values from -6 to 6
Outputs:
- layer_out: bfloat16 [128, 8, 1024], P('seq', 'dp', 'head'), parts along dimension 1
- grad_queries: bfloat16 [128, 8, 1024], P('seq', 'dp', 'head'), parts along dimension 1
- grad_gate: bfloat16 [128, 8, 1024], P('seq', 'dp', 'head'), parts along dimension 1
- grad_keys: bfloat16 [8192, 8, 1024], P('seq', 'dp', 'head'), parts along dimension 1
- grad_values: bfloat16 [8192, 8, 1024], P('seq', 'dp', 'head'), parts along dimension 1
The draws below stay inside these ranges and needn't reach their ends.
There are 2 independent parts, one for each index of `dp`. The reference program is written for one: setup_inputs(seed, part) draws one part's arguments, and reference() takes and returns one part's arrays. A program takes and returns all parts, laid end to end along the dimension named above; each array names one. Nothing has to cross between parts.
Inputs may be any that keep to these rules, and one draw needn't show every extreme that they name: Latent span c of user u names blocks (c - block_lists[c, u, i]) mod 8; the 4 entries of one row differ. Among the 4 rows of one latent span no offset occurs in more than 2 rows, and in some latent span one offset occurs in exactly 2 rows.
All inputs are finite; a program needn't handle non-finite values.
Results may differ from the reference program's by a relative error of at most 0.014.
Values may be sent and summed in bfloat16 or wider, within the bound.
A program may use at most 192 MiB of HBM per device.

```python
import math
import jax
import jax.numpy as jnp
import numpy as np
from jax import lax

HEADS = 16
HEAD_DIM = 64
D = 1024
USERS = 4
SPAN_ROWS = 16
BLOCK_ROWS = 1024
ENTRIES = 4
SLOTS = 2
LATENTS = 128
EVENTS = 8192
N_SEQ = 8


def plant(result, stream_key, low, high):
    longest = result.shape.index(max(result.shape))
    spots = []
    for shift in (0, 1):
        where = [jax.random.randint(jax.random.fold_in(stream_key, axis), (), 0, length) for axis, length in enumerate(result.shape)]
        where[longest] = (where[longest] + shift) % result.shape[longest]
        spots.append(tuple(where))
    return result.at[spots[0]].set(low).at[spots[1]].set(high)


def block_levels(own_key, extent, split, least, largest):
    level, own = 1.0, jax.random.fold_in(own_key, 6)
    for axis_at, shards_of in split:
        heights = jnp.exp(jax.random.uniform(jax.random.fold_in(own, axis_at), (shards_of,), jnp.float32, least / len(split), largest / len(split)))
        level = level * jnp.repeat(heights, extent[axis_at] // shards_of).reshape([-1 if axis == axis_at else 1 for axis in range(len(extent))])
    return level


def deal_out(rng, own, number, rows, amount, top, most, lean):
    ranking = jax.random.permutation(rng, amount)
    packed, ordinary = load_shares(amount, rows * top, most, lean, True), load_shares(amount, rows * top, most, lean, False)
    places = jnp.arange(amount)

    def named(tallies, offset_by):
        used = int((tallies > 0).sum())
        fixed = max(1, used // 4)
        shifted = fixed + (places - fixed + offset_by * (used - fixed)) % max(1, amount - fixed)
        return jnp.zeros((amount,), jnp.int32).at[ranking[jnp.where(places < fixed, places, shifted)]].set(jnp.asarray(tallies, jnp.int32))

    tallies = jnp.where(number % 4 == 0, named(packed, number // 4), named(ordinary, number - number // 4 - 1))
    mixed = jax.random.permutation(jax.random.fold_in(own, 3), amount)
    donor, taker = mixed[0:amount // 2 * 2:2], mixed[1:amount // 2 * 2:2]
    margin = jnp.minimum(tallies[donor] - 1, most - tallies[taker]) // 2
    margin = jnp.where((donor == ranking[0]) | (taker == ranking[0]) | (tallies[taker] == 0), 0, jnp.maximum(margin, 0))
    shifted = jax.random.randint(jax.random.fold_in(own, 4), (amount // 2,), 0, 1 << 20) % (margin + 1)
    tallies = tallies.at[donor].add(-shifted).at[taker].add(shifted)
    members = jnp.searchsorted(jnp.cumsum(tallies), jnp.arange(rows * top), side="right").astype(jnp.int32)
    grid = members.reshape(top, rows).T
    grid = grid[jax.random.permutation(jax.random.fold_in(own, 1), rows)]
    offset_by = jax.random.randint(jax.random.fold_in(own, 2), (rows, 1), 0, top)
    return jnp.take_along_axis(grid, (jnp.arange(top)[None, :] + offset_by) % top, axis=1)


def load_shares(number_of, total, bound, skew, full):
    portions = [(1 << 20) // math.isqrt(grade ** skew) + 1 for grade in range(1, number_of + 1)]
    largest = bound if full else min(bound, max(-(-total // number_of), total * portions[0] // sum(portions)))
    least = 1 if total - largest >= number_of - 1 else 0
    holding, surplus = [largest] + [least] * (number_of - 1), total - largest - least * (number_of - 1)
    while surplus > 0:
        movable = [i for i in range(1, number_of) if holding[i] < largest] or [i for i in range(1, number_of) if holding[i] < bound]
        whole, left = sum([portions[i] for i in movable]), surplus
        for i in movable:
            addition = min(bound - holding[i], max(1, left * portions[i] // whole), surplus)
            holding[i] = holding[i] + addition
            surplus = surplus - addition
    return np.array(holding)


def gaussian(own_key, dims, width, limit, shards=(), held_as=jnp.bfloat16):
    loudness = block_levels(own_key, dims, shards, -0.22, 0.18) if shards else 1.0
    array = jax.random.normal(own_key, dims, jnp.float32) * width * loudness
    return jnp.minimum(jnp.maximum(array, -limit), limit).astype(held_as)


def setup_inputs(seed: int = 0, part: int = 0) -> dict:
    streams_of = jax.random.split(jax.random.key(seed), 8)
    part_splits = jax.random.split(jax.random.fold_in(streams_of[7], part), 8)
    queries = gaussian(part_splits[0], (LATENTS, USERS, D), 1.0, 6.0, ((0, 8), (2, 2)))
    gate_pre = gaussian(part_splits[1], (LATENTS, USERS, D), 1.0, 6.0, ((0, 8), (2, 2)))
    event_keys = gaussian(part_splits[2], (EVENTS, USERS, D), 1.0, 6.0, ((0, 8), (2, 2)))
    event_values = gaussian(part_splits[3], (EVENTS, USERS, D), 1.0, 6.0, ((0, 8), (2, 2)))
    block_lists_keys = jax.random.split(jax.random.fold_in(part_splits[4], 1), N_SEQ * USERS // USERS)
    block_lists_turns = jax.random.permutation(jax.random.fold_in(part_splits[4], 3), N_SEQ * USERS // USERS)
    block_lists = jax.vmap(lambda own, number: deal_out(jax.random.fold_in(part_splits[4], 2), own, number, USERS, N_SEQ, ENTRIES, SLOTS, 2))(block_lists_keys, block_lists_turns).reshape((N_SEQ, USERS, ENTRIES))
    history_len = plant(jax.random.randint(part_splits[5], (USERS,), N_SEQ // 2, N_SEQ + 1), jax.random.fold_in(part_splits[5], 1), N_SEQ // 2, N_SEQ).astype(jnp.int32)
    out_grad = gaussian(part_splits[6], (LATENTS, USERS, D), 1.0, 6.0, ((0, 8), (2, 2)))
    return {"queries": queries, "gate_pre": gate_pre, "event_keys": event_keys, "event_values": event_values, "block_lists": block_lists, "history_len": history_len, "out_grad": out_grad}


EPS = 1e-06

def silu_slope(scores):
    logistic = jax.nn.sigmoid(scores)
    return logistic * (1.0 + scores * (1.0 - logistic))

def reference(queries, gate_pre, event_keys, event_values, block_lists, history_len, out_grad):
    factor = 1.0 / math.sqrt(HEAD_DIM)
    key_blocks = event_keys.reshape(N_SEQ, BLOCK_ROWS, USERS, D)
    value_blocks = event_values.reshape(N_SEQ, BLOCK_ROWS, USERS, D)
    user_ids = jnp.arange(USERS, dtype=jnp.int32)[:, None]

    def span_step(totals, span_index):
        key_total, value_total = totals
        first_row = span_index * SPAN_ROWS
        query_span = lax.dynamic_slice_in_dim(queries, first_row, SPAN_ROWS, 0)
        gate_value = lax.dynamic_slice_in_dim(gate_pre, first_row, SPAN_ROWS, 0).astype(jnp.float32)
        grad_out = lax.dynamic_slice_in_dim(out_grad, first_row, SPAN_ROWS, 0).astype(jnp.float32)
        gate_value = gate_value.reshape(SPAN_ROWS, USERS, HEADS, HEAD_DIM)
        grad_out = grad_out.reshape(SPAN_ROWS, USERS, HEADS, HEAD_DIM)
        offsets = lax.dynamic_index_in_dim(block_lists, span_index, 0, keepdims=False)
        blocks = ((span_index - offsets) % N_SEQ).astype(jnp.int32)
        usable = (blocks < history_len[:, None]).astype(jnp.float32)
        clipped = blocks
        key_heads = key_blocks[clipped, :, user_ids].astype(jnp.float32).reshape(USERS, ENTRIES * BLOCK_ROWS, HEADS, HEAD_DIM)
        value_heads = value_blocks[clipped, :, user_ids].astype(jnp.float32).reshape(USERS, ENTRIES * BLOCK_ROWS, HEADS, HEAD_DIM)
        key_mask = jnp.repeat(usable, BLOCK_ROWS, axis=1)[:, None, None, :]
        query_heads = query_span.astype(jnp.float32).reshape(SPAN_ROWS, USERS, HEADS, HEAD_DIM)
        scores = jnp.einsum('cuhd,ujhd->uhcj', query_heads, key_heads) * factor
        weights = (jax.nn.silu(scores) * key_mask).astype(jnp.bfloat16)
        attended = jnp.einsum('uhcj,ujhd->cuhd', weights.astype(jnp.float32), value_heads)
        inverse_root = lax.rsqrt(lax.optimization_barrier(jnp.mean(attended * attended, axis=-1, keepdims=True)) + EPS)
        normed = attended * inverse_root
        gate_silu = jax.nn.silu(gate_value)
        layer_out = (normed * gate_silu).astype(jnp.bfloat16)
        grad_gate = (grad_out * normed * silu_slope(gate_value)).astype(jnp.bfloat16)
        grad_normed = grad_out * gate_silu
        grad_attended = (inverse_root * (grad_normed - normed * lax.optimization_barrier(jnp.mean(grad_normed * normed, axis=-1, keepdims=True)))).astype(jnp.bfloat16)
        grad_heads = grad_attended.astype(jnp.float32)
        grad_weight = jnp.einsum('cuhd,ujhd->uhcj', grad_heads, value_heads)
        grad_scores = (grad_weight * silu_slope(scores) * factor * key_mask).astype(jnp.bfloat16)
        grad_query = jnp.einsum('uhcj,ujhd->cuhd', grad_scores.astype(jnp.float32), key_heads)
        key_part = jnp.einsum('uhcj,cuhd->ujhd', grad_scores.astype(jnp.float32), query_heads).reshape(USERS, ENTRIES, BLOCK_ROWS, D)
        value_part = jnp.einsum('uhcj,cuhd->ujhd', weights.astype(jnp.float32), grad_heads).reshape(USERS, ENTRIES, BLOCK_ROWS, D)
        key_total = key_total.at[clipped, :, user_ids].add(key_part)
        value_total = value_total.at[clipped, :, user_ids].add(value_part)
        shaped = (SPAN_ROWS, USERS, D)
        return ((key_total, value_total), (layer_out.reshape(shaped), grad_query.reshape(shaped).astype(jnp.bfloat16), grad_gate.reshape(shaped)))
    zero_total = jnp.zeros((N_SEQ, BLOCK_ROWS, USERS, D), jnp.float32)
    (key_total, value_total), stacked = lax.scan(span_step, (zero_total, zero_total), jnp.arange(N_SEQ, dtype=jnp.int32))
    layer_out = stacked[0].reshape(LATENTS, USERS, D)
    grad_queries = stacked[1].reshape(LATENTS, USERS, D)
    grad_gate = stacked[2].reshape(LATENTS, USERS, D)
    grad_keys = key_total.reshape(EVENTS, USERS, D).astype(jnp.bfloat16)
    grad_values = value_total.reshape(EVENTS, USERS, D).astype(jnp.bfloat16)
    return (layer_out, grad_queries, grad_gate, grad_keys, grad_values)
```

```python
import functools

import jax
import jax.numpy as jnp
from jax import lax
from jax.experimental import pallas as pl
from jax.experimental.pallas import tpu as pltpu
from jax.sharding import PartitionSpec as P

HEAD_DIM = 64
EPS = 1e-06
SLOTS = 2
PAIR = 2 * HEAD_DIM
TILE = 256
F32 = jnp.float32
BF16 = jnp.bfloat16
NT = (((1,), (1,)), ((), ()))
NN = (((1,), (0,)), ((), ()))


def dot(a, b, dims):
    return lax.dot_general(a, b, dims, preferred_element_type=F32)


def split_heads(rows):
    lane = lax.broadcasted_iota(jnp.int32, rows.shape, 1)
    zero = jnp.zeros_like(rows)
    return jnp.concatenate(
        [jnp.where(lane < HEAD_DIM, rows, zero), jnp.where(lane < HEAD_DIM, zero, rows)], axis=0
    )


def join_heads(flipped):
    half = flipped.shape[1] // 2
    return jnp.concatenate([flipped[:HEAD_DIM, :half], flipped[HEAD_DIM:, half:]], axis=0).T


def kernel(n, chunks, lists, lens, small, keys, values, small_out, dkeys, dvalues,
           k_buf, v_buf, kt_buf, vt_buf, w_buf, s_buf, q_dense, d_dense, a_dense, g_dense, d_own,
           sends, recvs,
           user_hold, slot_hold, user_own, slot_own,
           send_sem, recv_sem, load_sem, store_sem):
    users, events, width = k_buf.shape
    rows = small.shape[2]
    wide = width // chunks
    pairs = wide // PAIR
    latents = n * rows
    me = lax.axis_index("seq")

    def load_copy(i, u):
        src, dst = ((keys, k_buf), (values, v_buf))[i]
        return pltpu.make_async_copy(src.at[u], dst.at[u], load_sem.at[i, u])

    for u in range(users):
        load_copy(0, u).start()
        load_copy(1, u).start()

    barrier = pltpu.get_barrier_semaphore()

    def greet(d, carry):
        pl.semaphore_signal(barrier, inc=1, device_id={"seq": lax.rem(me + d, n)},
                            device_id_type=pl.DeviceIdType.MESH)
        return carry

    lax.fori_loop(1, n, greet, 0)

    def tables(p, carry):
        for user_of, slot_of, span, block in (
            (user_hold, slot_hold, p, me), (user_own, slot_own, me, p)
        ):
            offset = lax.rem(span - block + n, n)
            count = jnp.int32(0)
            named = [jnp.int32(0)] * SLOTS
            for u in range(users):
                hit = lists[span, u, 0] == offset
                for i in range(1, lists.shape[2]):
                    hit = hit | (lists[span, u, i] == offset)
                hit = hit & (block < lens[u])
                slot_of[p, u] = jnp.where(hit, count, SLOTS)
                for s in range(SLOTS):
                    named[s] = jnp.where(hit & (count == s), u, named[s])
                count = count + jnp.where(hit, 1, 0)
            for s in range(SLOTS):
                user_of[p, s] = named[s]
        return carry

    lax.fori_loop(0, n, tables, 0)

    for recv in recvs:
        for p in range(n):
            recv[p, SLOTS] = jnp.zeros((rows, wide), BF16)

    def copy(ph, f, to, slot):
        return pltpu.make_async_remote_copy(
            src_ref=sends.at[ph, f, to],
            dst_ref=recvs[ph * chunks + f].at[slot, pl.ds(0, SLOTS)],
            send_sem=send_sem.at[ph, f, to], recv_sem=recv_sem.at[ph, f, slot],
            device_id={"seq": to}, device_id_type=pl.DeviceIdType.MESH,
        )

    def exchange(ph, f, read, user_of):
        recv = recvs[ph * chunks + f]
        for s in range(SLOTS):
            recv[me, s] = read(user_of[me, s], me)

        def step(d, carry):
            to = lax.rem(me + d, n)
            for s in range(SLOTS):
                sends[ph, f, to, s] = read(user_of[to, s], to)
            copy(ph, f, to, me).start()
            return carry

        lax.fori_loop(1, n, step, 0)

    def arrive(ph, f):
        def step(d, carry):
            source = lax.rem(me + n - d, n)
            copy(ph, f, source, source).wait_recv()
            return carry

        lax.fori_loop(1, n, step, 0)

    def spread(ph, f, slot_of, dense):
        recv = recvs[ph * chunks + f]

        def step(p, carry):
            for u in range(users):
                dense[u, p, :, f * wide:(f + 1) * wide] = recv[p, slot_of[p, u]]
            return carry

        lax.fori_loop(0, n, step, 0)

    def gathered(ph, f, slot_of):
        recv = recvs[ph * chunks + f]
        out = []
        for u in range(users):
            total = recv[0, slot_of[0, u]].astype(F32)
            for p in range(1, n):
                total = total + recv[p, slot_of[p, u]].astype(F32)
            out.append(total)
        return jnp.concatenate(out, axis=0)

    def cols(f):
        return slice(f * wide, (f + 1) * wide)

    def each_pair(f, body):
        def step(i, carry):
            u = i // pairs
            at = pl.multiple_of(f * wide + lax.rem(i, pairs) * PAIR, PAIR)
            body(u, pl.ds(at, PAIR), f * users * pairs + i)
            return carry

        lax.fori_loop(0, users * pairs, step, 0)

    def forward(f):
        arrive(0, f)
        spread(0, f, slot_hold, q_dense)

        def body(u, at, index):
            query = split_heads(q_dense[u, :, :, at].reshape(latents, PAIR))
            for j in range(0, events, TILE):
                half = dot(k_buf[u, j:j + TILE, at], query, NT).astype(BF16)
                bent = jnp.tanh(half)
                up = 1.0 + bent
                weight = half * up
                w_buf[index, j:j + TILE] = weight
                s_buf[index, j:j + TILE] = up + weight * (1.0 - bent)
            a_dense[u, :, :, at] = join_heads(
                dot(vt_buf[u, at, :], w_buf[index], NN)
            ).astype(BF16).reshape(n, rows, PAIR)

        each_pair(f, body)
        exchange(1, f, lambda u, c: a_dense[u, c, :, cols(f)], user_hold)

    lane_a = lax.broadcasted_iota(jnp.int32, (PAIR, PAIR), 0) // HEAD_DIM
    lane_b = lax.broadcasted_iota(jnp.int32, (PAIR, PAIR), 1) // HEAD_DIM
    averager = jnp.where(lane_a == lane_b, 1.0 / HEAD_DIM, 0.0).astype(F32)

    def head_mean(x):
        return lax.dot_general(x, averager, NN, preferred_element_type=F32,
                               precision=lax.Precision.HIGHEST)

    def middle(f):
        arrive(1, f)
        attended_all = gathered(1, f, slot_own)
        for p in range(pairs):
            at = slice(f * wide + p * PAIR, f * wide + (p + 1) * PAIR)
            attended = attended_all[:, p * PAIR:(p + 1) * PAIR]
            gate = small[1, :, :, at].reshape(users * rows, PAIR).astype(F32)
            grad = small[2, :, :, at].reshape(users * rows, PAIR).astype(F32)
            root = lax.rsqrt(head_mean(attended * attended) + EPS)
            normed = attended * root
            logistic = jax.nn.sigmoid(gate)
            gate_silu = gate * logistic
            slope = logistic * (1.0 + gate * (1.0 - logistic))
            shape = (users, rows, PAIR)
            small_out[0, :, :, at] = (normed * gate_silu).astype(BF16).reshape(shape)
            small_out[2, :, :, at] = (grad * normed * slope).astype(BF16).reshape(shape)
            grad_normed = grad * gate_silu
            back = root * (grad_normed - normed * head_mean(grad_normed * normed))
            d_own[:, :, at] = back.astype(BF16).reshape(shape)
        exchange(2, f, lambda u, c: d_own[u, :, cols(f)], user_own)

    def store_copy(i, f, u):
        src, dst = ((k_buf, dkeys), (v_buf, dvalues))[i]
        return pltpu.make_async_copy(
            src.at[u, :, cols(f)], dst.at[u, :, cols(f)], store_sem.at[i, f, u])

    def backward(f):
        arrive(2, f)
        spread(2, f, slot_hold, d_dense)

        def body(u, at, index):
            query = split_heads(q_dense[u, :, :, at].reshape(latents, PAIR))
            grad = split_heads(d_dense[u, :, :, at].reshape(latents, PAIR))
            for j in range(0, events, TILE):
                tile = slice(j, j + TILE)
                grad_weight = dot(v_buf[u, tile, at], grad, NT).astype(BF16)
                grad_score = grad_weight * s_buf[index, tile]
                s_buf[index, tile] = grad_score
                v_buf[u, tile, at] = dot(w_buf[index, tile], grad, NN).astype(BF16)
                k_buf[u, tile, at] = dot(grad_score, query, NN).astype(BF16)
            g_dense[u, :, :, at] = (
                join_heads(dot(kt_buf[u, at, :], s_buf[index], NN)) * 0.0625
            ).astype(BF16).reshape(n, rows, PAIR)

        each_pair(f, body)
        exchange(3, f, lambda u, c: g_dense[u, c, :, cols(f)], user_hold)
        for u in range(users):
            store_copy(0, f, u).start()
            store_copy(1, f, u).start()

    def finish(f):
        arrive(3, f)
        small_out[1, :, :, cols(f)] = gathered(3, f, slot_own).astype(BF16).reshape(
            users, rows, wide)

    pl.semaphore_wait(barrier, n - 1)
    for f in range(chunks):
        exchange(0, f, lambda u, c: (small[0, u, :, cols(f)] * 0.0625).astype(BF16), user_own)

    for u in range(users):
        load_copy(0, u).wait()
        load_copy(1, u).wait()

    def flip(i, carry):
        u = i // (width // PAIR)
        at = pl.ds(pl.multiple_of(lax.rem(i, width // PAIR) * PAIR, PAIR), PAIR)
        kt_buf[u, at, :] = k_buf[u, :, at].T
        vt_buf[u, at, :] = v_buf[u, :, at].T
        return carry

    lax.fori_loop(0, users * (width // PAIR), flip, 0)

    forward(0)
    for f in range(1, chunks):
        forward(f)
        middle(f - 1)
    for f in range(chunks):
        if f == chunks - 1:
            middle(chunks - 1) if chunks == 1 else None
        backward(f)
        if f == 0 and chunks > 1:
            middle(chunks - 1)
    for f in range(chunks):
        finish(f)

    for ph in range(4):
        for f in range(chunks):
            def drain(d, carry):
                to = lax.rem(me + d, n)
                copy(ph, f, to, me).wait_send()
                return carry

            lax.fori_loop(1, n, drain, 0)
    for f in range(chunks):
        for u in range(users):
            store_copy(0, f, u).wait()
            store_copy(1, f, u).wait()


def body(n, chunks, queries, gate_pre, event_keys, event_values, block_lists, history_len, out_grad):
    rows, users, width = queries.shape
    events = event_keys.shape[0]
    small = jnp.stack([queries, gate_pre, out_grad]).transpose(0, 2, 1, 3)
    keys = event_keys.transpose(1, 0, 2)
    values = event_values.transpose(1, 0, 2)
    wide = width // chunks
    latents = n * rows
    pair_count = users * width // PAIR
    vmem = pl.BlockSpec(memory_space=pltpu.VMEM)
    smem = pl.BlockSpec(memory_space=pltpu.SMEM)
    hbm = pl.BlockSpec(memory_space=pl.ANY)
    table = [pltpu.SMEM((n, SLOTS), jnp.int32), pltpu.SMEM((n, users), jnp.int32)]
    flops = 6 * 2 * users * width * latents * events
    small_out, dkeys, dvalues = pl.pallas_call(
        functools.partial(kernel, n, chunks),
        out_shape=(
            jax.ShapeDtypeStruct((3, users, rows, width), BF16),
            jax.ShapeDtypeStruct((users, events, width), BF16),
            jax.ShapeDtypeStruct((users, events, width), BF16),
        ),
        in_specs=[smem, smem, vmem, hbm, hbm],
        out_specs=(vmem, hbm, hbm),
        scratch_shapes=[
            pltpu.VMEM((users, events, width), BF16),
            pltpu.VMEM((users, events, width), BF16),
            pltpu.VMEM((users, width, events), BF16),
            pltpu.VMEM((users, width, events), BF16),
            pltpu.VMEM((pair_count, events, 2 * latents), BF16),
            pltpu.VMEM((pair_count, events, 2 * latents), BF16),
            pltpu.VMEM((users, n, rows, width), BF16),
            pltpu.VMEM((users, n, rows, width), BF16),
            pltpu.VMEM((users, n, rows, width), BF16),
            pltpu.VMEM((users, n, rows, width), BF16),
            pltpu.VMEM((users, rows, width), BF16),
            pltpu.VMEM((4, chunks, n, SLOTS, rows, wide), BF16),
            (pltpu.VMEM((n, SLOTS + 1, rows, wide), BF16),) * (4 * chunks),
            *table,
            *table,
            pltpu.SemaphoreType.DMA((4, chunks, n)),
            pltpu.SemaphoreType.DMA((4, chunks, n)),
            pltpu.SemaphoreType.DMA((2, users)),
            pltpu.SemaphoreType.DMA((2, chunks, users)),
        ],
        compiler_params=pltpu.CompilerParams(
            collective_id=0, has_side_effects=True, vmem_limit_bytes=62 * 1024 * 1024
        ),
        cost_estimate=pl.CostEstimate(
            flops=flops, bytes_accessed=8 * users * events * width, transcendentals=0),
        name="sparse_attention",
    )(block_lists, history_len, small, keys, values)
    small_out = small_out.transpose(0, 2, 1, 3)
    return (
        small_out[0],
        small_out[1],
        small_out[2],
        dkeys.transpose(1, 0, 2),
        dvalues.transpose(1, 0, 2),
    )


def solution(mesh):
    shard = P("seq", "dp", "head")
    return jax.shard_map(
        functools.partial(body, mesh.shape["seq"], 2),
        mesh=mesh,
        in_specs=(shard, shard, shard, shard, P(None, "dp", None), P("dp"), shard),
        out_specs=(shard,) * 5,
        check_vma=False,
    )
```

```python
import functools

import jax
import jax.numpy as jnp
from jax import lax
from jax.experimental import pallas as pl
from jax.experimental.pallas import tpu as pltpu
from jax.sharding import PartitionSpec as P

HEAD_DIM = 64
EPS = 1e-06
SLOTS = 2
PAIR = 2 * HEAD_DIM
TILE = 256
GROUP = 64
F32 = jnp.float32
BF16 = jnp.bfloat16
NT = (((1,), (1,)), ((), ()))
NN = (((1,), (0,)), ((), ()))


def dot(a, b, dims):
    return lax.dot_general(a, b, dims, preferred_element_type=F32)


def split_heads(rows):
    lane = lax.broadcasted_iota(jnp.int32, rows.shape, 1)
    zero = jnp.zeros_like(rows)
    return jnp.concatenate(
        [jnp.where(lane < HEAD_DIM, rows, zero), jnp.where(lane < HEAD_DIM, zero, rows)], axis=0
    )


def join_heads(flipped):
    half = flipped.shape[1] // 2
    return jnp.concatenate([flipped[:HEAD_DIM, :half], flipped[HEAD_DIM:, half:]], axis=0).T


def kernel(n, chunks, lists, lens, queries, gates, grads, keys, values,
           out_rows, query_grads, gate_grads, dkeys, dvalues, raw, small, small_out, k_buf, v_buf, kt_buf, vt_buf, w_buf, s_buf, q_dense, d_dense, a_dense, d_own,
           sends, recvs,
           user_hold, slot_hold, user_own, slot_own,
           send_sem, recv_sem, load_sem, store_sem):
    users, events, width = k_buf.shape
    rows = queries.shape[0]
    wide = width // chunks
    pairs = wide // PAIR
    latents = n * rows
    me = lax.axis_index("seq")

    def cols(f):
        return slice(f * wide, (f + 1) * wide)

    def load_copy(i, f):
        return pltpu.make_async_copy(
            (keys, values)[i].at[:, :, cols(f)], raw.at[i, f % 2], load_sem.at[i, f])

    for f in range(min(2, chunks)):
        load_copy(0, f).start()
        load_copy(1, f).start()

    barrier = pltpu.get_barrier_semaphore()

    def greet(d, carry):
        pl.semaphore_signal(barrier, inc=1, device_id={"seq": lax.rem(me + d, n)},
                            device_id_type=pl.DeviceIdType.MESH)
        return carry

    lax.fori_loop(1, n, greet, 0)

    def tables(own, p, carry):
        for user_of, slot_of, span, block in (
            ((user_own, slot_own, me, p),) if own else ((user_hold, slot_hold, p, me),)
        ):
            offset = lax.rem(span - block + n, n)
            count = jnp.int32(0)
            named = [jnp.int32(0)] * SLOTS
            for u in range(users):
                hit = lists[u, 0, span] == offset
                for i in range(1, lists.shape[1]):
                    hit = hit | (lists[u, i, span] == offset)
                hit = hit & (block < lens[u])
                slot_of[p, u] = jnp.where(hit, count, SLOTS)
                for s in range(SLOTS):
                    named[s] = jnp.where(hit & (count == s), u, named[s])
                count = count + jnp.where(hit, 1, 0)
            for s in range(SLOTS):
                user_of[p, s] = named[s]
        return carry

    lax.fori_loop(0, n, functools.partial(tables, True), 0)
    small[0] = (jnp.swapaxes(queries[...], 0, 1) * 0.0625).astype(BF16)

    for recv in recvs:
        for p in range(n):
            recv[p, SLOTS] = jnp.zeros((rows, wide), BF16)

    def copy(ph, f, to, slot):
        return pltpu.make_async_remote_copy(
            src_ref=sends.at[ph, f, to],
            dst_ref=recvs[ph * chunks + f].at[slot, pl.ds(0, SLOTS)],
            send_sem=send_sem.at[ph, f, to], recv_sem=recv_sem.at[ph, f, slot],
            device_id={"seq": to}, device_id_type=pl.DeviceIdType.MESH,
        )

    def exchange(ph, f, read, user_of):
        recv = recvs[ph * chunks + f]
        for s in range(SLOTS):
            recv[me, s] = read(user_of[me, s], me)

        def step(d, carry):
            to = lax.rem(me + d, n)
            for s in range(SLOTS):
                sends[ph, f, to, s] = read(user_of[to, s], to)
            copy(ph, f, to, me).start()
            return carry

        lax.fori_loop(1, n, step, 0)

    def arrive(ph, f):
        def step(d, carry):
            source = lax.rem(me + n - d, n)
            copy(ph, f, source, source).wait_recv()
            return carry

        lax.fori_loop(1, n, step, 0)

    def spread(ph, f, slot_of, dense):
        recv = recvs[ph * chunks + f]

        def step(p, carry):
            for u in range(users):
                dense[u, p, :, f * wide:(f + 1) * wide] = recv[p, slot_of[p, u]]
            return carry

        lax.fori_loop(0, n, step, 0)

    def gathered(ph, f, slot_of):
        recv = recvs[ph * chunks + f]
        out = []
        for u in range(users):
            total = recv[0, slot_of[0, u]].astype(F32)
            for p in range(1, n):
                total = total + recv[p, slot_of[p, u]].astype(F32)
            out.append(total)
        return jnp.concatenate(out, axis=0)

    def each_pair(f, body):
        def step(i, carry):
            u = i // pairs
            at = pl.multiple_of(f * wide + lax.rem(i, pairs) * PAIR, PAIR)
            body(u, pl.ds(at, PAIR), f * users * pairs + i)
            return carry

        lax.fori_loop(0, users * pairs, step, 0)

    def forward(f):
        arrive(0, f)
        spread(0, f, slot_hold, q_dense)

        def body(u, at, index):
            query = split_heads(q_dense[u, :, :, at].reshape(latents, PAIR))
            for j in range(0, events, TILE):
                half = dot(k_buf[u, j:j + TILE, at], query, NT).astype(BF16)
                bent = jnp.tanh(half)
                up = 1.0 + bent
                weight = half * up
                w_buf[index, j:j + TILE] = weight
                s_buf[index, j:j + TILE] = up + weight * (1.0 - bent)
            a_dense[u, :, :, at] = join_heads(
                dot(vt_buf[u, at, :], w_buf[index], NN)
            ).astype(BF16).reshape(n, rows, PAIR)

        each_pair(f, body)
        exchange(1, f, lambda u, c: a_dense[u, c, :, cols(f)], user_hold)

    lane_a = lax.broadcasted_iota(jnp.int32, (PAIR, PAIR), 0) // HEAD_DIM
    lane_b = lax.broadcasted_iota(jnp.int32, (PAIR, PAIR), 1) // HEAD_DIM
    averager = jnp.where(lane_a == lane_b, 1.0 / HEAD_DIM, 0.0).astype(F32)

    def head_mean(x):
        return lax.dot_general(x, averager, NN, preferred_element_type=F32,
                               precision=lax.Precision.HIGHEST)

    def middle(f):
        arrive(1, f)
        attended_all = gathered(1, f, slot_own)
        for p in range(pairs):
            at = slice(f * wide + p * PAIR, f * wide + (p + 1) * PAIR)
            attended = attended_all[:, p * PAIR:(p + 1) * PAIR]
            gate = small[1, :, :, at].reshape(users * rows, PAIR).astype(F32)
            grad = small[2, :, :, at].reshape(users * rows, PAIR).astype(F32)
            root = lax.rsqrt(head_mean(attended * attended) + EPS)
            normed = attended * root
            logistic = jax.nn.sigmoid(gate)
            gate_silu = gate * logistic
            slope = logistic * (1.0 + gate * (1.0 - logistic))
            shape = (users, rows, PAIR)
            small_out[0, :, :, at] = (normed * gate_silu).astype(BF16).reshape(shape)
            small_out[2, :, :, at] = (grad * normed * slope).astype(BF16).reshape(shape)
            grad_normed = grad * gate_silu
            back = root * (grad_normed - normed * head_mean(grad_normed * normed))
            d_own[:, :, at] = back.astype(BF16).reshape(shape)
        exchange(2, f, lambda u, c: d_own[u, :, cols(f)], user_own)

    def store_copy(i, f):
        return pltpu.make_async_copy(
            raw.at[i, f % 2], (dkeys, dvalues)[i].at[:, :, cols(f)], store_sem.at[i, f])

    def prepare(f):
        for i, buf in enumerate((k_buf, v_buf)):
            load_copy(i, f).wait()

            def split(g, carry):
                at = pl.ds(pl.multiple_of(g * GROUP, GROUP), GROUP)
                buf[:, at, cols(f)] = jnp.swapaxes(raw[i, f % 2, at], 0, 1)
                return carry

            lax.fori_loop(0, events // GROUP, split, 0)
            if f + 2 < chunks:
                load_copy(i, f + 2).start()

        def flip(u, at, index):
            kt_buf[u, at, :] = k_buf[u, :, at].T
            vt_buf[u, at, :] = v_buf[u, :, at].T

        each_pair(f, flip)

    def backward(f):
        arrive(2, f)
        spread(2, f, slot_hold, d_dense)

        def body(u, at, index):
            query = split_heads(q_dense[u, :, :, at].reshape(latents, PAIR))
            grad = split_heads(d_dense[u, :, :, at].reshape(latents, PAIR))
            for j in range(0, events, TILE):
                tile = slice(j, j + TILE)
                grad_weight = dot(v_buf[u, tile, at], grad, NT).astype(BF16)
                grad_score = grad_weight * s_buf[index, tile]
                s_buf[index, tile] = grad_score
                v_buf[u, tile, at] = dot(w_buf[index, tile], grad, NN).astype(BF16)
                k_buf[u, tile, at] = dot(grad_score, query, NN).astype(BF16)
            a_dense[u, :, :, at] = (
                join_heads(dot(kt_buf[u, at, :], s_buf[index], NN)) * 0.0625
            ).astype(BF16).reshape(n, rows, PAIR)

        each_pair(f, body)
        exchange(3, f, lambda u, c: a_dense[u, c, :, cols(f)], user_hold)
        for i, buf in enumerate((k_buf, v_buf)):
            if f >= 2:
                store_copy(i, f - 2).wait()

            def merge(g, carry):
                at = pl.ds(pl.multiple_of(g * GROUP, GROUP), GROUP)
                raw[i, f % 2, at] = jnp.swapaxes(buf[:, at, cols(f)], 0, 1)
                return carry

            lax.fori_loop(0, events // GROUP, merge, 0)
            store_copy(i, f).start()

    def finish(f):
        arrive(3, f)
        small_out[1, :, :, cols(f)] = gathered(3, f, slot_own).astype(BF16).reshape(
            users, rows, wide)

    pl.semaphore_wait(barrier, n - 1)
    for f in range(chunks):
        exchange(0, f, lambda u, c: small[0, u, :, cols(f)], user_own)

    small[1] = jnp.swapaxes(gates[...], 0, 1)
    small[2] = jnp.swapaxes(grads[...], 0, 1)
    lax.fori_loop(0, n, functools.partial(tables, False), 0)

    prepare(0)
    forward(0)
    for f in range(1, chunks):
        prepare(f)
        forward(f)
        middle(f - 1)
    if chunks == 1:
        middle(0)
    for f in range(chunks):
        backward(f)
        if f == 0 and chunks > 1:
            middle(chunks - 1)
        if f > 0:
            finish(f - 1)
    finish(chunks - 1)
    for ref, i in ((out_rows, 0), (query_grads, 1), (gate_grads, 2)):
        ref[...] = jnp.swapaxes(small_out[i], 0, 1)

    for ph in range(4):
        for f in range(chunks):
            def drain(d, carry):
                to = lax.rem(me + d, n)
                copy(ph, f, to, me).wait_send()
                return carry

            lax.fori_loop(1, n, drain, 0)
    for f in range(max(0, chunks - 2), chunks):
        store_copy(0, f).wait()
        store_copy(1, f).wait()


def body(n, chunks, queries, gate_pre, event_keys, event_values, block_lists, history_len, out_grad):
    rows, users, width = queries.shape
    events = event_keys.shape[0]
    wide = width // chunks
    latents = n * rows
    pair_count = users * width // PAIR
    vmem = pl.BlockSpec(memory_space=pltpu.VMEM)
    smem = pl.BlockSpec(memory_space=pltpu.SMEM)
    hbm = pl.BlockSpec(memory_space=pl.ANY)
    table = [pltpu.SMEM((n, SLOTS), jnp.int32), pltpu.SMEM((n, users), jnp.int32)]
    flops = 6 * 2 * users * width * latents * events
    return pl.pallas_call(
        functools.partial(kernel, n, chunks),
        out_shape=(
            *(jax.ShapeDtypeStruct((rows, users, width), BF16),) * 3,
            jax.ShapeDtypeStruct((events, users, width), BF16),
            jax.ShapeDtypeStruct((events, users, width), BF16),
        ),
        in_specs=[smem, smem, vmem, vmem, vmem, hbm, hbm],
        out_specs=(vmem, vmem, vmem, hbm, hbm),
        scratch_shapes=[
            pltpu.VMEM((2, 2, events, users, wide), BF16),
            pltpu.VMEM((3, users, rows, width), BF16),
            pltpu.VMEM((3, users, rows, width), BF16),
            pltpu.VMEM((users, events, width), BF16),
            pltpu.VMEM((users, events, width), BF16),
            pltpu.VMEM((users, width, events), BF16),
            pltpu.VMEM((users, width, events), BF16),
            pltpu.VMEM((pair_count, events, 2 * latents), BF16),
            pltpu.VMEM((pair_count, events, 2 * latents), BF16),
            pltpu.VMEM((users, n, rows, width), BF16),
            pltpu.VMEM((users, n, rows, width), BF16),
            pltpu.VMEM((users, n, rows, width), BF16),
            pltpu.VMEM((users, rows, width), BF16),
            pltpu.VMEM((4, chunks, n, SLOTS, rows, wide), BF16),
            (pltpu.VMEM((n, SLOTS + 1, rows, wide), BF16),) * (4 * chunks),
            *table,
            *table,
            pltpu.SemaphoreType.DMA((4, chunks, n)),
            pltpu.SemaphoreType.DMA((4, chunks, n)),
            pltpu.SemaphoreType.DMA((2, chunks)),
            pltpu.SemaphoreType.DMA((2, chunks)),
        ],
        compiler_params=pltpu.CompilerParams(
            collective_id=0, has_side_effects=True, vmem_limit_bytes=62 * 1024 * 1024
        ),
        cost_estimate=pl.CostEstimate(
            flops=flops, bytes_accessed=8 * users * events * width, transcendentals=0),
        name="sparse_attention",
    )(block_lists.transpose(1, 2, 0), history_len, queries, gate_pre, out_grad,
      event_keys, event_values)


def solution(mesh):
    shard = P("seq", "dp", "head")
    return jax.shard_map(
        functools.partial(body, mesh.shape["seq"], 4),
        mesh=mesh,
        in_specs=(shard, shard, shard, shard, P(None, "dp", None), P("dp"), shard),
        out_specs=(shard,) * 5,
        check_vma=False,
    )
```

```python
import functools

import jax
import jax.numpy as jnp
from jax import lax
from jax.experimental import pallas as pl
from jax.experimental.pallas import tpu as pltpu
from jax.sharding import PartitionSpec as P

HEAD_DIM = 64
EPS = 1e-06
SLOTS = 2
PAIR = 2 * HEAD_DIM
TILE = 256
GROUP = 64
F32 = jnp.float32
BF16 = jnp.bfloat16
NT = (((1,), (1,)), ((), ()))
NN = (((1,), (0,)), ((), ()))


def dot(a, b, dims):
    return lax.dot_general(a, b, dims, preferred_element_type=F32)


def split_heads(rows):
    lane = lax.broadcasted_iota(jnp.int32, rows.shape, 1)
    zero = jnp.zeros_like(rows)
    return jnp.concatenate(
        [jnp.where(lane < HEAD_DIM, rows, zero), jnp.where(lane < HEAD_DIM, zero, rows)], axis=0
    )


def join_heads(flipped):
    half = flipped.shape[1] // 2
    return jnp.concatenate([flipped[:HEAD_DIM, :half], flipped[HEAD_DIM:, half:]], axis=0).T


def kernel(n, chunks, lists, lens, queries, gates, grads, keys, values,
           small_out, dkeys, dvalues, raw, small, k_buf, v_buf, kt_buf, vt_buf, w_buf, s_buf, q_dense, d_dense, a_dense, d_own,
           sends, recvs,
           user_hold, slot_hold, user_own, slot_own,
           send_sem, recv_sem, load_sem, store_sem):
    users, events, width = k_buf.shape
    rows = queries.shape[0]
    wide = width // chunks
    pairs = wide // PAIR
    latents = n * rows
    me = lax.axis_index("seq")

    def cols(f):
        return slice(f * wide, (f + 1) * wide)

    def load_copy(i, f):
        return pltpu.make_async_copy(
            (keys, values)[i].at[:, :, cols(f)], raw.at[i, f % 2], load_sem.at[i, f])

    for f in range(min(2, chunks)):
        load_copy(0, f).start()
        load_copy(1, f).start()

    barrier = pltpu.get_barrier_semaphore()

    def greet(d, carry):
        pl.semaphore_signal(barrier, inc=1, device_id={"seq": lax.rem(me + d, n)},
                            device_id_type=pl.DeviceIdType.MESH)
        return carry

    lax.fori_loop(1, n, greet, 0)

    def tables(own, p, carry):
        for user_of, slot_of, span, block in (
            ((user_own, slot_own, me, p),) if own else ((user_hold, slot_hold, p, me),)
        ):
            offset = lax.rem(span - block + n, n)
            count = jnp.int32(0)
            named = [jnp.int32(0)] * SLOTS
            for u in range(users):
                hit = lists[u, 0, span] == offset
                for i in range(1, lists.shape[1]):
                    hit = hit | (lists[u, i, span] == offset)
                hit = hit & (block < lens[u])
                slot_of[p, u] = jnp.where(hit, count, SLOTS)
                for s in range(SLOTS):
                    named[s] = jnp.where(hit & (count == s), u, named[s])
                count = count + jnp.where(hit, 1, 0)
            for s in range(SLOTS):
                user_of[p, s] = named[s]
        return carry

    lax.fori_loop(0, n, functools.partial(tables, True), 0)
    small[0] = (jnp.swapaxes(queries[...], 0, 1) * 0.0625).astype(BF16)

    for recv in recvs:
        for p in range(n):
            recv[p, SLOTS] = jnp.zeros((rows, wide), BF16)

    def copy(ph, f, to, slot):
        return pltpu.make_async_remote_copy(
            src_ref=sends.at[ph, f, to],
            dst_ref=recvs[ph * chunks + f].at[slot, pl.ds(0, SLOTS)],
            send_sem=send_sem.at[ph, f, to], recv_sem=recv_sem.at[ph, f, slot],
            device_id={"seq": to}, device_id_type=pl.DeviceIdType.MESH,
        )

    def exchange(ph, f, read, user_of):
        recv = recvs[ph * chunks + f]
        for s in range(SLOTS):
            recv[me, s] = read(user_of[me, s], me)

        def step(d, carry):
            to = lax.rem(me + d, n)
            for s in range(SLOTS):
                sends[ph, f, to, s] = read(user_of[to, s], to)
            copy(ph, f, to, me).start()
            return carry

        lax.fori_loop(1, n, step, 0)

    def arrive(ph, f):
        def step(d, carry):
            source = lax.rem(me + n - d, n)
            copy(ph, f, source, source).wait_recv()
            return carry

        lax.fori_loop(1, n, step, 0)

    def spread(ph, f, slot_of, dense):
        recv = recvs[ph * chunks + f]

        def step(p, carry):
            for u in range(users):
                dense[u, p, :, f * wide:(f + 1) * wide] = recv[p, slot_of[p, u]]
            return carry

        lax.fori_loop(0, n, step, 0)

    def gathered(ph, f, slot_of):
        recv = recvs[ph * chunks + f]
        out = []
        for u in range(users):
            total = recv[0, slot_of[0, u]].astype(F32)
            for p in range(1, n):
                total = total + recv[p, slot_of[p, u]].astype(F32)
            out.append(total)
        return jnp.concatenate(out, axis=0)

    def each_pair(f, body):
        def step(i, carry):
            u = i // pairs
            at = pl.multiple_of(f * wide + lax.rem(i, pairs) * PAIR, PAIR)
            body(u, pl.ds(at, PAIR), f * users * pairs + i)
            return carry

        lax.fori_loop(0, users * pairs, step, 0)

    def forward(f):
        arrive(0, f)
        spread(0, f, slot_hold, q_dense)

        def body(u, at, index):
            query = split_heads(q_dense[u, :, :, at].reshape(latents, PAIR))
            for j in range(0, events, TILE):
                half = dot(k_buf[u, j:j + TILE, at], query, NT).astype(BF16)
                bent = jnp.tanh(half)
                up = 1.0 + bent
                weight = half * up
                w_buf[index, j:j + TILE] = weight
                s_buf[index, j:j + TILE] = up + weight * (1.0 - bent)
            a_dense[u, :, :, at] = join_heads(
                dot(vt_buf[u, at, :], w_buf[index], NN)
            ).astype(BF16).reshape(n, rows, PAIR)

        each_pair(f, body)
        exchange(1, f, lambda u, c: a_dense[u, c, :, cols(f)], user_hold)

    lane_a = lax.broadcasted_iota(jnp.int32, (PAIR, PAIR), 0) // HEAD_DIM
    lane_b = lax.broadcasted_iota(jnp.int32, (PAIR, PAIR), 1) // HEAD_DIM
    averager = jnp.where(lane_a == lane_b, 1.0 / HEAD_DIM, 0.0).astype(F32)

    def head_mean(x):
        return lax.dot_general(x, averager, NN, preferred_element_type=F32,
                               precision=lax.Precision.HIGHEST)

    def middle(f):
        arrive(1, f)
        attended_all = gathered(1, f, slot_own)
        for p in range(pairs):
            at = slice(f * wide + p * PAIR, f * wide + (p + 1) * PAIR)
            attended = attended_all[:, p * PAIR:(p + 1) * PAIR]
            gate = small[1, :, :, at].reshape(users * rows, PAIR).astype(F32)
            grad = small[2, :, :, at].reshape(users * rows, PAIR).astype(F32)
            root = lax.rsqrt(head_mean(attended * attended) + EPS)
            normed = attended * root
            logistic = jax.nn.sigmoid(gate)
            gate_silu = gate * logistic
            slope = logistic * (1.0 + gate * (1.0 - logistic))
            shape = (users, rows, PAIR)
            small_out[0, :, :, at] = (normed * gate_silu).astype(BF16).reshape(shape)
            small_out[2, :, :, at] = (grad * normed * slope).astype(BF16).reshape(shape)
            grad_normed = grad * gate_silu
            back = root * (grad_normed - normed * head_mean(grad_normed * normed))
            d_own[:, :, at] = back.astype(BF16).reshape(shape)
        exchange(2, f, lambda u, c: d_own[u, :, cols(f)], user_own)

    def store_copy(i, f):
        return pltpu.make_async_copy(
            raw.at[i, f % 2], (dkeys, dvalues)[i].at[:, :, cols(f)], store_sem.at[i, f])

    def prepare(f):
        for i, buf in enumerate((k_buf, v_buf)):
            load_copy(i, f).wait()

            def split(g, carry):
                at = pl.ds(pl.multiple_of(g * GROUP, GROUP), GROUP)
                buf[:, at, cols(f)] = jnp.swapaxes(raw[i, f % 2, at], 0, 1)
                return carry

            lax.fori_loop(0, events // GROUP, split, 0)
            if f + 2 < chunks:
                load_copy(i, f + 2).start()

        def flip(u, at, index):
            kt_buf[u, at, :] = k_buf[u, :, at].T
            vt_buf[u, at, :] = v_buf[u, :, at].T

        each_pair(f, flip)

    def backward(f):
        arrive(2, f)
        spread(2, f, slot_hold, d_dense)

        def body(u, at, index):
            query = split_heads(q_dense[u, :, :, at].reshape(latents, PAIR))
            grad = split_heads(d_dense[u, :, :, at].reshape(latents, PAIR))
            for j in range(0, events, TILE):
                tile = slice(j, j + TILE)
                grad_weight = dot(v_buf[u, tile, at], grad, NT).astype(BF16)
                grad_score = grad_weight * s_buf[index, tile]
                s_buf[index, tile] = grad_score
                v_buf[u, tile, at] = dot(w_buf[index, tile], grad, NN).astype(BF16)
                k_buf[u, tile, at] = dot(grad_score, query, NN).astype(BF16)
            a_dense[u, :, :, at] = (
                join_heads(dot(kt_buf[u, at, :], s_buf[index], NN)) * 0.0625
            ).astype(BF16).reshape(n, rows, PAIR)

        each_pair(f, body)
        exchange(3, f, lambda u, c: a_dense[u, c, :, cols(f)], user_hold)
        for i, buf in enumerate((k_buf, v_buf)):
            if f >= 2:
                store_copy(i, f - 2).wait()

            def merge(g, carry):
                at = pl.ds(pl.multiple_of(g * GROUP, GROUP), GROUP)
                raw[i, f % 2, at] = jnp.swapaxes(buf[:, at, cols(f)], 0, 1)
                return carry

            lax.fori_loop(0, events // GROUP, merge, 0)
            store_copy(i, f).start()

    def finish(f):
        arrive(3, f)
        small_out[1, :, :, cols(f)] = gathered(3, f, slot_own).astype(BF16).reshape(
            users, rows, wide)

    pl.semaphore_wait(barrier, n - 1)
    for f in range(chunks):
        exchange(0, f, lambda u, c: small[0, u, :, cols(f)], user_own)

    small[1] = jnp.swapaxes(gates[...], 0, 1)
    small[2] = jnp.swapaxes(grads[...], 0, 1)
    lax.fori_loop(0, n, functools.partial(tables, False), 0)

    prepare(0)
    forward(0)
    for f in range(1, chunks):
        prepare(f)
        forward(f)
        middle(f - 1)
    if chunks == 1:
        middle(0)
    for f in range(chunks):
        backward(f)
        if f == 0 and chunks > 1:
            middle(chunks - 1)
        if f > 0:
            finish(f - 1)
    finish(chunks - 1)

    for ph in range(4):
        for f in range(chunks):
            def drain(d, carry):
                to = lax.rem(me + d, n)
                copy(ph, f, to, me).wait_send()
                return carry

            lax.fori_loop(1, n, drain, 0)
    for f in range(max(0, chunks - 2), chunks):
        store_copy(0, f).wait()
        store_copy(1, f).wait()


def body(n, chunks, queries, gate_pre, event_keys, event_values, block_lists, history_len, out_grad):
    rows, users, width = queries.shape
    events = event_keys.shape[0]
    wide = width // chunks
    latents = n * rows
    pair_count = users * width // PAIR
    vmem = pl.BlockSpec(memory_space=pltpu.VMEM)
    smem = pl.BlockSpec(memory_space=pltpu.SMEM)
    hbm = pl.BlockSpec(memory_space=pl.ANY)
    table = [pltpu.SMEM((n, SLOTS), jnp.int32), pltpu.SMEM((n, users), jnp.int32)]
    flops = 6 * 2 * users * width * latents * events
    small_out, dkeys, dvalues = pl.pallas_call(
        functools.partial(kernel, n, chunks),
        out_shape=(
            jax.ShapeDtypeStruct((3, users, rows, width), BF16),
            jax.ShapeDtypeStruct((events, users, width), BF16),
            jax.ShapeDtypeStruct((events, users, width), BF16),
        ),
        in_specs=[smem, smem, vmem, vmem, vmem, hbm, hbm],
        out_specs=(vmem, hbm, hbm),
        scratch_shapes=[
            pltpu.VMEM((2, 2, events, users, wide), BF16),
            pltpu.VMEM((3, users, rows, width), BF16),
            pltpu.VMEM((users, events, width), BF16),
            pltpu.VMEM((users, events, width), BF16),
            pltpu.VMEM((users, width, events), BF16),
            pltpu.VMEM((users, width, events), BF16),
            pltpu.VMEM((pair_count, events, 2 * latents), BF16),
            pltpu.VMEM((pair_count, events, 2 * latents), BF16),
            pltpu.VMEM((users, n, rows, width), BF16),
            pltpu.VMEM((users, n, rows, width), BF16),
            pltpu.VMEM((users, n, rows, width), BF16),
            pltpu.VMEM((users, rows, width), BF16),
            pltpu.VMEM((4, chunks, n, SLOTS, rows, wide), BF16),
            (pltpu.VMEM((n, SLOTS + 1, rows, wide), BF16),) * (4 * chunks),
            *table,
            *table,
            pltpu.SemaphoreType.DMA((4, chunks, n)),
            pltpu.SemaphoreType.DMA((4, chunks, n)),
            pltpu.SemaphoreType.DMA((2, chunks)),
            pltpu.SemaphoreType.DMA((2, chunks)),
        ],
        compiler_params=pltpu.CompilerParams(
            collective_id=0, has_side_effects=True, vmem_limit_bytes=62 * 1024 * 1024
        ),
        cost_estimate=pl.CostEstimate(
            flops=flops, bytes_accessed=8 * users * events * width, transcendentals=0),
        name="sparse_attention",
    )(block_lists.transpose(1, 2, 0), history_len, queries, gate_pre, out_grad,
      event_keys, event_values)
    small_out = small_out.transpose(0, 2, 1, 3)
    return small_out[0], small_out[1], small_out[2], dkeys, dvalues


def solution(mesh):
    shard = P("seq", "dp", "head")
    return jax.shard_map(
        functools.partial(body, mesh.shape["seq"], 4),
        mesh=mesh,
        in_specs=(shard, shard, shard, shard, P(None, "dp", None), P("dp"), shard),
        out_specs=(shard,) * 5,
        check_vma=False,
    )
```
